32 devices in a mesh: grp: 4 (over z), ep: 8 (over y, x, core), tp: 1.
Axes of the slice: x: 2, y: 2, z: 4, core: 2. Of those that a mesh axis runs over, the one named last changes fastest.
Arguments:
- tokens: bfloat16 [4096, 2048], P(('grp', 'ep'), 'tp'), may hold values from -6 to 6
- expert_ids: int32 [4096, 4], P(('grp', 'ep')), may hold values from 0 to 31, all different within a row; in each aligned block of 128 rows (0 to 127, 128 to 255, ...) at most 24 rows name the same one
- router_probs: float32 [4096, 4], P(('grp', 'ep')), may hold values from 0.02 to 1
- cotangent: bfloat16 [4096, 2048], P(('grp', 'ep'), 'tp'), may hold values from -6 to 6
- w_gate: bfloat16 [32, 2048, 768], P(('grp', 'ep'), None, 'tp'), may hold values from -0.125 to 0.125
- w_up: bfloat16 [32, 2048, 768], P(('grp', 'ep'), None, 'tp'), may hold values from -0.125 to 0.125
- w_down: bfloat16 [32, 768, 2048], P(('grp', 'ep'), 'tp'), may hold values from -0.21875 to 0.21875
Outputs:
- layer_out: bfloat16 [4096, 2048], P(('grp', 'ep'), 'tp')
- grad_tokens: bfloat16 [4096, 2048], P(('grp', 'ep'), 'tp')
- grad_gate: bfloat16 [32, 2048, 768], P(('grp', 'ep'), None, 'tp')
- grad_up: bfloat16 [32, 2048, 768], P(('grp', 'ep'), None, 'tp')
- grad_down: bfloat16 [32, 768, 2048], P(('grp', 'ep'), 'tp')
The draws below stay inside these ranges and needn't reach their ends.
Inputs may be any that keep to these rules, and one draw needn't show every extreme that they name: `expert_ids`: each token names 4 different experts. Among the 128 rows of one index of grp+ep no expert is named by more than 24 tokens, and in some such block one expert is named by exactly 24.
All inputs are finite; a program needn't handle non-finite values.
Results may differ from the reference program's by a relative error of at most 0.0085.
Values may be sent and summed in bfloat16 or wider, within the bound.
A program may use at most 128 MiB of HBM per device.

```python
import math
import jax
import jax.numpy as jnp
import numpy as np
from jax import lax

D = 2048
FF = 768
TOK_DEV = 128
TOPK = 4
EXPERTS = 32
CAP = 24
SLOTS = 768
TOKENS = 4096


def levels(own_key, shape, split, least, largest):
    gain, own = 1.0, jax.random.fold_in(own_key, 6)
    for axis_at, shards_of in split:
        heights = jnp.exp(jax.random.uniform(jax.random.fold_in(own, axis_at), (shards_of,), jnp.float32, least / len(split), largest / len(split)))
        gain = gain * jnp.repeat(heights, shape[axis_at] // shards_of).reshape([-1 if axis == axis_at else 1 for axis in range(len(shape))])
    return gain


def assign_block(stream_key, own, number, rows, count, top, reach, slope):
    ranking = jax.random.permutation(stream_key, count)
    crowded, common = shares(count, rows * top, reach, slope, True), shares(count, rows * top, reach, slope, False)
    places = jnp.arange(count)

    def named(tallies, turn):
        used = int((tallies > 0).sum())
        fixed = max(1, used // 4)
        shifted = fixed + (places - fixed + turn * (used - fixed)) % max(1, count - fixed)
        return jnp.zeros((count,), jnp.int32).at[ranking[jnp.where(places < fixed, places, shifted)]].set(jnp.asarray(tallies, jnp.int32))

    tallies = jnp.where(number % 4 == 0, named(crowded, number // 4), named(common, number - number // 4 - 1))
    mixed = jax.random.permutation(jax.random.fold_in(own, 3), count)
    donor, receiver = mixed[0:count // 2 * 2:2], mixed[1:count // 2 * 2:2]
    room = jnp.minimum(tallies[donor] - 1, reach - tallies[receiver]) // 2
    room = jnp.where((donor == ranking[0]) | (receiver == ranking[0]) | (tallies[receiver] == 0), 0, jnp.maximum(room, 0))
    shifted = jax.random.randint(jax.random.fold_in(own, 4), (count // 2,), 0, 1 << 20) % (room + 1)
    tallies = tallies.at[donor].add(-shifted).at[receiver].add(shifted)
    members = jnp.searchsorted(jnp.cumsum(tallies), jnp.arange(rows * top), side="right").astype(jnp.int32)
    listing = members.reshape(top, rows).T
    listing = listing[jax.random.permutation(jax.random.fold_in(own, 1), rows)]
    turn = jax.random.randint(jax.random.fold_in(own, 2), (rows, 1), 0, top)
    return jnp.take_along_axis(listing, (jnp.arange(top)[None, :] + turn) % top, axis=1)


def shares(count, total, limit, skew, full):
    loads = [(1 << 20) // math.isqrt(rank ** skew) + 1 for rank in range(1, count + 1)]
    largest = limit if full else min(limit, max(-(-total // count), total * loads[0] // sum(loads)))
    least = 1 if total - largest >= count - 1 else 0
    given, rest = [largest] + [least] * (count - 1), total - largest - least * (count - 1)
    while rest > 0:
        movable = [i for i in range(1, count) if given[i] < largest] or [i for i in range(1, count) if given[i] < limit]
        whole, left = sum([loads[i] for i in movable]), rest
        for i in movable:
            addition = min(limit - given[i], max(1, left * loads[i] // whole), rest)
            given[i] = given[i] + addition
            rest = rest - addition
    return np.array(given)


def centred(own_key, dims, width, most, split=(), kind=jnp.bfloat16):
    gain = levels(own_key, dims, split, -0.22, 0.18) if split else 1.0
    result = jax.random.normal(own_key, dims, jnp.float32) * width * gain
    return jnp.minimum(jnp.maximum(result, -most), most).astype(kind)


def setup_inputs(seed: int = 0) -> dict:
    arg_keys = jax.random.split(jax.random.key(seed), 8)
    tokens = centred(arg_keys[0], (TOKENS, D), 1.0, 6.0, ((0, 32),))
    expert_ids_keys = jax.random.split(jax.random.fold_in(arg_keys[1], 1), TOKENS // TOK_DEV)
    expert_ids_turns = jax.random.permutation(jax.random.fold_in(arg_keys[1], 3), TOKENS // TOK_DEV)
    expert_ids = jax.vmap(lambda own, number: assign_block(jax.random.fold_in(arg_keys[1], 2), own, number, TOK_DEV, EXPERTS, TOPK, CAP, 2))(expert_ids_keys, expert_ids_turns).reshape((TOKENS, TOPK))
    router_probs = jnp.clip(jnp.exp(math.log(1.0) - 3.912023 * jax.random.uniform(arg_keys[2], (TOKENS, TOPK), jnp.float32) ** levels(arg_keys[2], (TOKENS, TOPK), ((0, 32),), -0.2, 0.2)), 0.02, 1.0)
    cotangent = centred(arg_keys[3], (TOKENS, D), 1.0, 6.0, ((0, 32),))
    w_gate = centred(arg_keys[4], (EXPERTS, D, FF), D ** -0.5, 0.125, ((0, 32),))
    w_up = centred(arg_keys[5], (EXPERTS, D, FF), D ** -0.5, 0.125, ((0, 32),))
    w_down = centred(arg_keys[6], (EXPERTS, FF, D), FF ** -0.5, 0.21875, ((0, 32),))
    return {"tokens": tokens, "expert_ids": expert_ids, "router_probs": router_probs, "cotangent": cotangent, "w_gate": w_gate, "w_up": w_up, "w_down": w_down}


def reference(tokens, expert_ids, router_probs, cotangent, w_gate, w_up, w_down):
    combine = router_probs / jnp.sum(router_probs, axis=1, keepdims=True)
    flat_ids = expert_ids.reshape(-1)
    flat_weight = combine.reshape(-1)
    flat_token = (jnp.arange(TOKENS * TOPK) // TOPK).astype(jnp.int32)
    places = jnp.arange(SLOTS).astype(jnp.int32)

    def per_expert(carry, expert):
        out_total, grad_total = carry
        matches = flat_ids == expert
        where_rows = jnp.nonzero(matches, size=SLOTS, fill_value=0)[0].astype(jnp.int32)
        is_live = (places < jnp.sum(matches.astype(jnp.int32)).astype(jnp.int32)).astype(jnp.float32)
        token_rows = flat_token[where_rows]
        row_weight = flat_weight[where_rows] * is_live
        inputs = tokens[token_rows]
        gate_pre = jnp.dot(inputs, w_gate[expert], preferred_element_type=jnp.float32)
        up_pre = jnp.dot(inputs, w_up[expert], preferred_element_type=jnp.float32)
        sigmoid_gate = jax.nn.sigmoid(gate_pre)
        activated = gate_pre * sigmoid_gate
        hidden = (activated * up_pre).astype(jnp.bfloat16)
        expert_out = jnp.dot(hidden, w_down[expert], preferred_element_type=jnp.float32).astype(jnp.bfloat16)
        grad_row = (row_weight[:, None] * cotangent[token_rows].astype(jnp.float32)).astype(jnp.bfloat16)
        grad_hidden = jnp.dot(grad_row, w_down[expert].T, preferred_element_type=jnp.float32)
        grad_gate_pre = (grad_hidden * up_pre * sigmoid_gate * (1.0 + gate_pre * (1.0 - sigmoid_gate))).astype(jnp.bfloat16)
        grad_up_pre = (grad_hidden * activated).astype(jnp.bfloat16)
        grad_down_e = jnp.dot(hidden.T, grad_row, preferred_element_type=jnp.float32).astype(jnp.bfloat16)
        grad_gate_e = jnp.dot(inputs.T, grad_gate_pre, preferred_element_type=jnp.float32).astype(jnp.bfloat16)
        grad_up_e = jnp.dot(inputs.T, grad_up_pre, preferred_element_type=jnp.float32).astype(jnp.bfloat16)
        grad_row_in = (jnp.dot(grad_gate_pre, w_gate[expert].T, preferred_element_type=jnp.float32)
                       + jnp.dot(grad_up_pre, w_up[expert].T, preferred_element_type=jnp.float32)).astype(jnp.bfloat16)
        out_total = out_total.at[token_rows].add(row_weight[:, None] * expert_out.astype(jnp.float32))
        grad_total = grad_total.at[token_rows].add(is_live[:, None] * grad_row_in.astype(jnp.float32))
        return (out_total, grad_total), (grad_gate_e, grad_up_e, grad_down_e)

    start = (jnp.zeros((TOKENS, D), jnp.float32), jnp.zeros((TOKENS, D), jnp.float32))
    expert_list = jnp.arange(EXPERTS).astype(jnp.int32)
    (out_total, grad_total), (grad_gate, grad_up, grad_down) = lax.scan(per_expert, start, expert_list)
    return (out_total.astype(jnp.bfloat16), grad_total.astype(jnp.bfloat16), grad_gate, grad_up, grad_down)
```

```python
import jax
import jax.numpy as jnp
from jax import lax
from jax.sharding import PartitionSpec as P

F32 = jnp.float32
BF16 = jnp.bfloat16


def expert_math(rows_full, grads_full, gate_local, up_local, down_local):
    contract_last = (((1,), (1,)), ((), ()))
    contract_first = (((0,), (0,)), ((), ()))
    gate_pre = jnp.dot(rows_full, gate_local, preferred_element_type=F32)
    up_pre = jnp.dot(rows_full, up_local, preferred_element_type=F32)
    sigmoid_gate = jax.nn.sigmoid(gate_pre)
    activated = gate_pre * sigmoid_gate
    hidden = (activated * up_pre).astype(BF16)
    out_partial = jnp.dot(hidden, down_local, preferred_element_type=F32)
    grad_hidden = lax.dot_general(grads_full, down_local, contract_last, preferred_element_type=F32)
    grad_gate_pre = (
        grad_hidden * up_pre * sigmoid_gate * (1.0 + gate_pre * (1.0 - sigmoid_gate))
    ).astype(BF16)
    grad_up_pre = (grad_hidden * activated).astype(BF16)
    input_partial = lax.dot_general(
        grad_gate_pre, gate_local, contract_last, preferred_element_type=F32
    ) + lax.dot_general(grad_up_pre, up_local, contract_last, preferred_element_type=F32)
    down_grad = lax.dot_general(hidden, grads_full, contract_first, preferred_element_type=F32)
    gate_grad = lax.dot_general(rows_full, grad_gate_pre, contract_first, preferred_element_type=F32)
    up_grad = lax.dot_general(rows_full, grad_up_pre, contract_first, preferred_element_type=F32)
    return (out_partial, input_partial, gate_grad, up_grad, down_grad)


def on_device(tokens, expert_ids, router_probs, cotangent, w_gate, w_up, w_down):
    groups = lax.axis_size("grp")
    plane = lax.axis_size("ep")
    experts = groups * plane
    tok_rows, width = tokens.shape
    top_count = expert_ids.shape[1]
    capacity = 3 * tok_rows * top_count // (2 * experts)
    combine = router_probs / jnp.sum(router_probs, axis=1, keepdims=True)
    packed = jnp.concatenate([expert_ids.astype(F32), combine], axis=1)
    packed_all = lax.all_gather(packed, "grp", axis=0, tiled=False)
    tokens_all = lax.all_gather(tokens, "grp", axis=0, tiled=False)
    cot_all = lax.all_gather(cotangent, "grp", axis=0, tiled=False)
    ids_all = packed_all[:, :, :top_count]
    weight_all = packed_all[:, :, top_count:]
    mine = lax.axis_index("grp") * plane + jnp.arange(plane, dtype=jnp.int32)
    hits = ids_all[None] == mine.astype(F32)[:, None, None, None]
    member = jnp.any(hits, axis=3)
    weight = jnp.sum(jnp.where(hits, weight_all[None], 0.0), axis=3)
    count = member.astype(jnp.int32)
    rank = jnp.cumsum(count, axis=2) - count
    slots = jnp.arange(capacity, dtype=jnp.int32)
    chosen = jnp.logical_and(
        rank[:, :, None, :] == slots[None, None, :, None], member[:, :, None, :]
    )
    select_bf = chosen.astype(BF16)
    weighted = jnp.where(chosen, weight[:, :, None, :], 0.0)
    slot_weight = jnp.sum(weighted, axis=3)
    weight_bf = weighted.astype(BF16)

    def spread(blocks):
        return jnp.einsum("ezst,ztd->ezsd", select_bf, blocks, preferred_element_type=F32)

    def swap(rows):
        return lax.all_to_all(rows, "ep", split_axis=0, concat_axis=0, tiled=True)

    sent_rows = spread(tokens_all).astype(BF16)
    sent_grads = (slot_weight[..., None] * spread(cot_all)).astype(BF16)
    flat = (experts * capacity, width)
    rows_full = lax.all_gather(swap(sent_rows).reshape(flat), "tp", axis=1, tiled=True)
    grads_full = lax.all_gather(swap(sent_grads).reshape(flat), "tp", axis=1, tiled=True)
    out_partial, input_partial, gate_grad, up_grad, down_grad = expert_math(
        rows_full, grads_full, w_gate[0], w_up[0], w_down[0]
    )
    out_half = lax.psum_scatter(out_partial, "tp", scatter_dimension=1, tiled=True)
    input_half = lax.psum_scatter(input_partial, "tp", scatter_dimension=1, tiled=True)
    shape = (plane, groups, capacity, width)

    def gather_back(rows, select):
        back = swap(rows.astype(BF16).reshape(shape))
        part = jnp.einsum("ezst,ezsd->ztd", select, back, preferred_element_type=F32)
        part = part.astype(BF16).reshape(groups * tok_rows, width)
        return lax.psum_scatter(part, "grp", scatter_dimension=0, tiled=True)

    layer_out = gather_back(out_half, weight_bf)
    grad_tokens = gather_back(input_half, select_bf)
    return (
        layer_out.astype(BF16),
        grad_tokens.astype(BF16),
        gate_grad.astype(BF16)[None],
        up_grad.astype(BF16)[None],
        down_grad.astype(BF16)[None],
    )


def solution(mesh):
    return jax.shard_map(
        on_device,
        mesh=mesh,
        in_specs=(
            P(("grp", "ep"), "tp"),
            P(("grp", "ep"), None),
            P(("grp", "ep"), None),
            P(("grp", "ep"), "tp"),
            P(("grp", "ep"), None, "tp"),
            P(("grp", "ep"), None, "tp"),
            P(("grp", "ep"), "tp", None),
        ),
        out_specs=(
            P(("grp", "ep"), "tp"),
            P(("grp", "ep"), "tp"),
            P(("grp", "ep"), None, "tp"),
            P(("grp", "ep"), None, "tp"),
            P(("grp", "ep"), "tp", None),
        ),
        check_vma=False,
    )
```

```python
import functools

import jax
import jax.numpy as jnp
from jax import lax
from jax.experimental import pallas as pl
from jax.experimental.pallas import tpu as pltpu
from jax.sharding import PartitionSpec as P

F32 = jnp.float32
BF16 = jnp.bfloat16
MESH = pl.DeviceIdType.MESH


def expert_math(rows_full, grads_full, gate_local, up_local, down_local):
    contract_last = (((1,), (1,)), ((), ()))
    contract_first = (((0,), (0,)), ((), ()))
    gate_pre = jnp.dot(rows_full, gate_local, preferred_element_type=F32)
    up_pre = jnp.dot(rows_full, up_local, preferred_element_type=F32)
    sigmoid_gate = jax.nn.sigmoid(gate_pre)
    activated = gate_pre * sigmoid_gate
    hidden = (activated * up_pre).astype(BF16)
    out_partial = jnp.dot(hidden, down_local, preferred_element_type=F32)
    grad_hidden = lax.dot_general(grads_full, down_local, contract_last, preferred_element_type=F32)
    grad_gate_pre = (
        grad_hidden * up_pre * sigmoid_gate * (1.0 + gate_pre * (1.0 - sigmoid_gate))
    ).astype(BF16)
    grad_up_pre = (grad_hidden * activated).astype(BF16)
    input_partial = lax.dot_general(
        grad_gate_pre, gate_local, contract_last, preferred_element_type=F32
    ) + lax.dot_general(grad_up_pre, up_local, contract_last, preferred_element_type=F32)
    down_grad = lax.dot_general(hidden, grads_full, contract_first, preferred_element_type=F32)
    gate_grad = lax.dot_general(rows_full, grad_gate_pre, contract_first, preferred_element_type=F32)
    up_grad = lax.dot_general(rows_full, grad_up_pre, contract_first, preferred_element_type=F32)
    return (out_partial, input_partial, gate_grad, up_grad, down_grad)


def block_at(g, groups, i):
    low, high = g, groups - 1 - g
    near = jnp.minimum(low, high)
    inside = i <= 2 * near
    far = i - near
    half = (i + 1) // 2
    odd = lax.rem(i, 2)
    side_in = 1 - 2 * odd
    side_out = jnp.where(low < high, 1, -1)
    return g + jnp.where(inside, side_in * half, side_out * far)


def greet(groups, plane):
    g, me = lax.axis_index("grp"), lax.axis_index("ep")
    barrier = pltpu.get_barrier_semaphore()

    def signal_peer(j, carry):
        pl.semaphore_signal(
            barrier, inc=1, device_id={"ep": lax.rem(me + j, plane)}, device_id_type=MESH
        )
        return carry

    lax.fori_loop(1, plane, signal_peer, 0)

    @pl.when(g > 0)
    def _():
        pl.semaphore_signal(barrier, inc=1, device_id={"grp": g - 1}, device_id_type=MESH)

    @pl.when(g < groups - 1)
    def _():
        pl.semaphore_signal(barrier, inc=1, device_id={"grp": g + 1}, device_id_type=MESH)

    beside = jnp.minimum(g, 1) + jnp.minimum(groups - 1 - g, 1)
    pl.semaphore_wait(barrier, plane - 1 + beside)


def remote(src, dst, send, recv, device):
    return pltpu.make_async_remote_copy(
        src_ref=src, dst_ref=dst, send_sem=send, recv_sem=recv,
        device_id=device, device_id_type=MESH,
    )


def dispatch_kernel(
    groups, plane, capacity, top,
    meta_ref, tok_ref, cot_ref,
    rows_ref, grads_ref, select_ref, weight_ref,
    meta, blocks, stage, slot_w,
    own_sem, meta_send, meta_recv, up_send, down_send, z_recv, row_send, row_recv, self_sem,
):
    g, me = lax.axis_index("grp"), lax.axis_index("ep")
    tok_rows, width = tok_ref.shape
    chunk = min(width, 512)
    arrived = (rows_ref, grads_ref)
    own = [
        pltpu.make_async_copy(meta_ref, meta.at[g], own_sem.at[2]),
        pltpu.make_async_copy(tok_ref, blocks.at[0, g], own_sem.at[0]),
        pltpu.make_async_copy(cot_ref, blocks.at[1, g], own_sem.at[1]),
    ]
    for copy in own:
        copy.start()
    greet(groups, plane)
    for copy in own:
        copy.wait()

    def up_meta(s):
        return remote(meta.at[s], meta.at[s], meta_send.at[0, s], meta_recv.at[s], {"grp": g + 1})

    def down_meta(s):
        return remote(meta.at[s], meta.at[s], meta_send.at[1, s], meta_recv.at[s], {"grp": g - 1})

    def up_block(a, s):
        block = blocks.at[a, s]
        return remote(block, block, up_send.at[a, s], z_recv.at[a, s], {"grp": g + 1})

    def down_block(a, s):
        block = blocks.at[a, s]
        return remote(block, block, down_send.at[a, s], z_recv.at[a, s], {"grp": g - 1})

    def row_copy(a, s, j):
        e = lax.rem(me + j, plane)
        return remote(
            stage.at[a, s, e], arrived[a].at[me, s], row_send.at[a, s, j],
            row_recv.at[a, me, s], {"ep": e},
        )

    def self_copy(a, s):
        return pltpu.make_async_copy(
            stage.at[a, s, me], arrived[a].at[me, s], self_sem.at[a, s]
        )

    def goes_up(s):
        return jnp.logical_and(s <= g, g < groups - 1)

    def goes_down(s):
        return jnp.logical_and(s >= g, g > 0)

    def select_rows(s):
        info = meta[s]
        expert = g * plane + lax.broadcasted_iota(jnp.int32, (plane, tok_rows), 0)
        expert = expert.astype(F32)
        member = jnp.zeros((plane, tok_rows), F32)
        weight = jnp.zeros((plane, tok_rows), F32)
        for k in range(top):
            hit = info[k:k + 1, :] == expert
            member = jnp.where(hit, 1.0, member)
            weight = jnp.where(hit, info[top + k:top + k + 1, :], weight)
        earlier = lax.broadcasted_iota(jnp.int32, (tok_rows, tok_rows), 0)
        later = lax.broadcasted_iota(jnp.int32, (tok_rows, tok_rows), 1)
        before = jnp.where(earlier < later, 1.0, 0.0).astype(BF16)
        rank = jnp.dot(member.astype(BF16), before, preferred_element_type=F32)
        place = jnp.where(member > 0.0, rank, -1.0)
        slots = lax.broadcasted_iota(jnp.int32, (capacity, tok_rows), 0).astype(F32)
        picked, scaled = [], []
        for e in range(plane):
            chosen = place[e:e + 1, :] == slots
            picked.append(jnp.where(chosen, 1.0, 0.0))
            scaled.append(jnp.where(chosen, weight[e:e + 1, :], 0.0))
        picked, scaled = jnp.concatenate(picked, axis=0), jnp.concatenate(scaled, axis=0)
        select_ref[s] = picked.astype(BF16)
        weight_ref[s] = scaled.astype(BF16)
        slot_w[s] = jnp.sum(scaled, axis=1, keepdims=True)

    for a in range(2):

        def step(i, carry, a=a):
            s = block_at(g, groups, i)
            if a == 0:
                @pl.when(i > 0)
                def _():
                    down_meta(s).wait_recv()

                @pl.when(goes_up(s))
                def _():
                    up_meta(s).start()

                @pl.when(goes_down(s))
                def _():
                    down_meta(s).start()

            @pl.when(i > 0)
            def _():
                down_block(a, s).wait_recv()

            @pl.when(goes_up(s))
            def _():
                up_block(a, s).start()

            @pl.when(goes_down(s))
            def _():
                down_block(a, s).start()

            if a == 0:
                select_rows(s)
            for at in range(0, width, chunk):
                part = jnp.dot(
                    select_ref[s], blocks[a, s, :, at:at + chunk], preferred_element_type=F32
                )
                if a == 1:
                    part = part * slot_w[s]
                for e in range(plane):
                    stage[a, s, e, :, at:at + chunk] = part[
                        e * capacity:(e + 1) * capacity, :
                    ].astype(BF16)

            def send(j, inner):
                row_copy(a, s, j).start()
                return inner

            lax.fori_loop(1, plane, send, 0)
            self_copy(a, s).start()
            return carry

        lax.fori_loop(0, groups, step, 0)

    for a in range(2):

        def drain(s, carry, a=a):
            if a == 0:
                @pl.when(goes_up(s))
                def _():
                    up_meta(s).wait_send()

                @pl.when(goes_down(s))
                def _():
                    down_meta(s).wait_send()

            @pl.when(goes_up(s))
            def _():
                up_block(a, s).wait_send()

            @pl.when(goes_down(s))
            def _():
                down_block(a, s).wait_send()

            self_copy(a, s).wait()

            def finish(j, inner):
                e = lax.rem(me + j, plane)
                row_copy(a, s, j).wait_send()
                remote(
                    stage.at[a, s, e], arrived[a].at[e, s], row_send.at[a, s, j],
                    row_recv.at[a, e, s], {"ep": e},
                ).wait_recv()
                return inner

            lax.fori_loop(1, plane, finish, 0)
            return carry

        lax.fori_loop(0, groups, drain, 0)


def dispatch(groups, plane, capacity, top, meta, tokens, cotangent):
    tok_rows, width = tokens.shape
    slots = plane * capacity
    arrived = jax.ShapeDtypeStruct((plane, groups, capacity, width), BF16)
    chosen = jax.ShapeDtypeStruct((groups, slots, tok_rows), BF16)
    dma = pltpu.SemaphoreType.DMA
    return pl.pallas_call(
        functools.partial(dispatch_kernel, groups, plane, capacity, top),
        out_shape=(arrived, arrived, chosen, chosen),
        in_specs=[pl.BlockSpec(memory_space=pl.ANY)] * 3,
        out_specs=(pl.BlockSpec(memory_space=pl.ANY),) * 2
        + (pl.BlockSpec(memory_space=pltpu.VMEM),) * 2,
        scratch_shapes=[
            pltpu.VMEM((groups,) + meta.shape, F32),
            pltpu.VMEM((2, groups, tok_rows, width), BF16),
            pltpu.VMEM((2, groups, plane, capacity, width), BF16),
            pltpu.VMEM((groups, slots, 1), F32),
            dma((3,)), dma((2, groups)), dma((groups,)),
            dma((2, groups)), dma((2, groups)), dma((2, groups)),
            dma((2, groups, plane)), dma((2, plane, groups)), dma((2, groups)),
        ],
        compiler_params=pltpu.CompilerParams(
            collective_id=0, has_side_effects=True, vmem_limit_bytes=60 * 1024 * 1024
        ),
    )(meta, tokens, cotangent)


def combine_kernel(
    groups, plane, capacity,
    out_ref, inp_ref, select_ref, weight_ref,
    layer_ref, grad_ref,
    back, partial, from_low, from_high,
    row_send, row_recv, self_sem, up_send, down_send, low_recv, high_recv,
):
    g, me = lax.axis_index("grp"), lax.axis_index("ep")
    tok_rows, width = layer_ref.shape
    chunk = min(width, 512)
    sources, results, selects = (out_ref, inp_ref), (layer_ref, grad_ref), (weight_ref, select_ref)

    def row_copy(a, d, j):
        e = lax.rem(me + j, plane)
        return remote(
            sources[a].at[e, d], back.at[a, d, me], row_send.at[a, d, j],
            row_recv.at[a, me, d], {"ep": e},
        )

    def self_copy(a, d):
        return pltpu.make_async_copy(
            sources[a].at[me, d], back.at[a, d, me], self_sem.at[a, d]
        )

    def up_copy(a, d):
        return remote(
            partial.at[a, d], from_low.at[a, d], up_send.at[a, d], low_recv.at[a, d],
            {"grp": g + 1},
        )

    def down_copy(a, d):
        return remote(
            partial.at[a, d], from_high.at[a, d], down_send.at[a, d], high_recv.at[a, d],
            {"grp": g - 1},
        )

    greet(groups, plane)
    for a in range(2):

        def launch(i, carry, a=a):
            d = block_at(g, groups, groups - 1 - i)

            def send(j, inner):
                row_copy(a, d, j).start()
                return inner

            lax.fori_loop(1, plane, send, 0)
            self_copy(a, d).start()
            return carry

        lax.fori_loop(0, groups, launch, 0)

    for a in range(2):

        def step(i, carry, a=a):
            d = block_at(g, groups, groups - 1 - i)
            self_copy(a, d).wait()

            def arrive(j, inner):
                e = lax.rem(me + j, plane)
                row_copy(a, d, j).wait_send()
                remote(
                    sources[a].at[e, d], back.at[a, d, e], row_send.at[a, d, j],
                    row_recv.at[a, e, d], {"ep": e},
                ).wait_recv()
                return inner

            lax.fori_loop(1, plane, arrive, 0)
            has_low = jnp.logical_and(d >= g, g > 0)
            has_high = jnp.logical_and(d <= g, g < groups - 1)

            @pl.when(has_low)
            def _():
                up_copy(a, d).wait_recv()

            @pl.when(has_high)
            def _():
                down_copy(a, d).wait_recv()

            @pl.when(jnp.logical_not(has_low))
            def _():
                from_low[a, d] = jnp.zeros((tok_rows, width), BF16)

            @pl.when(jnp.logical_not(has_high))
            def _():
                from_high[a, d] = jnp.zeros((tok_rows, width), BF16)

            for at in range(0, width, chunk):
                cols = slice(at, at + chunk)
                rows = jnp.concatenate(
                    [back[a, d, e, :, cols].astype(F32) for e in range(plane)], axis=0
                ).astype(BF16)
                part = lax.dot_general(
                    selects[a][d], rows, (((0,), (0,)), ((), ())), preferred_element_type=F32
                )
                part = part + from_low[a, d, :, cols].astype(F32)
                part = part + from_high[a, d, :, cols].astype(F32)
                partial[a, d, :, cols] = part.astype(BF16)

            @pl.when(d > g)
            def _():
                up_copy(a, d).start()

            @pl.when(d < g)
            def _():
                down_copy(a, d).start()

            return carry

        lax.fori_loop(0, groups, step, 0)
        results[a][...] = partial[a, g]

    for a in range(2):

        def drain(d, carry, a=a):
            @pl.when(d > g)
            def _():
                up_copy(a, d).wait_send()

            @pl.when(d < g)
            def _():
                down_copy(a, d).wait_send()

            return carry

        lax.fori_loop(0, groups, drain, 0)


def gather_back(groups, plane, capacity, out_rows, in_rows, select, weight):
    tok_rows, width = select.shape[2], out_rows.shape[3]
    result = jax.ShapeDtypeStruct((tok_rows, width), BF16)
    dma = pltpu.SemaphoreType.DMA
    blocks = pltpu.VMEM((2, groups, tok_rows, width), BF16)
    return pl.pallas_call(
        functools.partial(combine_kernel, groups, plane, capacity),
        out_shape=(result, result),
        in_specs=[pl.BlockSpec(memory_space=pl.ANY)] * 2
        + [pl.BlockSpec(memory_space=pltpu.VMEM)] * 2,
        out_specs=(pl.BlockSpec(memory_space=pltpu.VMEM),) * 2,
        scratch_shapes=[
            pltpu.VMEM((2, groups, plane, capacity, width), BF16),
            blocks, blocks, blocks,
            dma((2, groups, plane)), dma((2, plane, groups)), dma((2, groups)),
            dma((2, groups)), dma((2, groups)), dma((2, groups)), dma((2, groups)),
        ],
        compiler_params=pltpu.CompilerParams(
            collective_id=1, has_side_effects=True, vmem_limit_bytes=60 * 1024 * 1024
        ),
    )(out_rows, in_rows, select, weight)


def on_device(tokens, expert_ids, router_probs, cotangent, w_gate, w_up, w_down):
    groups = lax.axis_size("grp")
    plane = lax.axis_size("ep")
    experts = groups * plane
    tok_rows, width = tokens.shape
    top = expert_ids.shape[1]
    capacity = -(-3 * tok_rows * top // (2 * experts) // 8) * 8
    combine = router_probs / jnp.sum(router_probs, axis=1, keepdims=True)
    meta = jnp.concatenate([expert_ids.astype(F32), combine], axis=1).T
    rows, grads, select, weight = dispatch(
        groups, plane, capacity, top, meta, tokens, cotangent
    )
    flat = (experts * capacity, width)
    rows_full = lax.all_gather(rows.reshape(flat), "tp", axis=1, tiled=True)
    grads_full = lax.all_gather(grads.reshape(flat), "tp", axis=1, tiled=True)
    out_partial, input_partial, gate_grad, up_grad, down_grad = expert_math(
        rows_full, grads_full, w_gate[0], w_up[0], w_down[0]
    )
    out_half = lax.psum_scatter(out_partial, "tp", scatter_dimension=1, tiled=True)
    input_half = lax.psum_scatter(input_partial, "tp", scatter_dimension=1, tiled=True)
    shape = (plane, groups, capacity, width)
    layer_out, grad_tokens = gather_back(
        groups, plane, capacity,
        out_half.astype(BF16).reshape(shape), input_half.astype(BF16).reshape(shape),
        select, weight,
    )
    return (
        layer_out,
        grad_tokens,
        gate_grad.astype(BF16)[None],
        up_grad.astype(BF16)[None],
        down_grad.astype(BF16)[None],
    )


def solution(mesh):
    return jax.shard_map(
        on_device,
        mesh=mesh,
        in_specs=(
            P(("grp", "ep"), "tp"),
            P(("grp", "ep"), None),
            P(("grp", "ep"), None),
            P(("grp", "ep"), "tp"),
            P(("grp", "ep"), None, "tp"),
            P(("grp", "ep"), None, "tp"),
            P(("grp", "ep"), "tp", None),
        ),
        out_specs=(
            P(("grp", "ep"), "tp"),
            P(("grp", "ep"), "tp"),
            P(("grp", "ep"), None, "tp"),
            P(("grp", "ep"), None, "tp"),
            P(("grp", "ep"), "tp", None),
        ),
        check_vma=False,
    )
```
